32 devices in a mesh: mom: 8 (over z, x), tm: 4 (over y, core).
Axes of the slice: x: 2, y: 2, z: 4, core: 2. Of those that a mesh axis runs over, the one named last changes fastest.
Arguments:
- new_rows: float32 [4, 256, 16, 512], P(None, 'mom', None, 'tm'), may hold values from -9 to 9
- history: float32 [3, 2, 256, 512, 512], P(None, None, 'mom', 'tm'), may hold values from -0.25 to 0.25
- momentum_map: int32 [256], replicated, may hold values from 0 to 255, each once
- step_index: int32 [1], replicated, may hold values from 0 to 999
- history_len: int32 [1], replicated, may hold values from 256 to 512
Outputs:
- advanced_rows: float32 [4, 256, 16, 512], P(None, 'mom', None, 'tm')
The draws below stay inside these ranges and needn't reach their ends.
Inputs may be any that keep to these rules, and one draw needn't show every extreme that they name: `momentum_map`: each number of 0 to 255 appears once.
All inputs are finite; a program needn't handle non-finite values.
Results may differ from the reference program's by a relative error of at most 0.0003.
Values sent between devices are 32-bit elements; how exact they have to be, the bound alone decides.
A program may use at most 256 MiB of HBM per device.

```python
import jax
import jax.numpy as jnp
from jax import lax

SIDE = 16
MOMENTA = 256
HIST = 512
ROWS = 16


def levels(rng, extent, pieces, low, largest):
    loudness, own = 1.0, jax.random.fold_in(rng, 6)
    for dim, shards_of in pieces:
        steps = jnp.exp(jax.random.uniform(jax.random.fold_in(own, dim), (shards_of,), jnp.float32, low / len(pieces), largest / len(pieces)))
        loudness = loudness * jnp.repeat(steps, extent[dim] // shards_of).reshape([-1 if axis == dim else 1 for axis in range(len(extent))])
    return loudness


def noise(rng, shape, spread, reach, split=(), kind=jnp.bfloat16):
    factor_of = levels(rng, shape, split, -0.22, 0.18) if split else 1.0
    array = jax.random.normal(rng, shape, jnp.float32) * spread * factor_of
    return jnp.minimum(jnp.maximum(array, -reach), reach).astype(kind)


def setup_inputs(seed: int = 0) -> dict:
    splits = jax.random.split(jax.random.key(seed), 6)
    return {
        "new_rows": noise(splits[0], (4, MOMENTA, ROWS, HIST), 1.5, 9.0, ((1, 8), (3, 4)), jnp.float32),
        "history": noise(splits[1], (3, 2, MOMENTA, HIST, HIST), HIST ** -0.5, 0.25, ((2, 8), (3, 4)), jnp.float32),
        "momentum_map": jax.random.permutation(splits[2], MOMENTA).astype(jnp.int32),
        "step_index": jax.random.randint(splits[3], (1,), 0, 1000).astype(jnp.int32),
        "history_len": jax.random.randint(splits[4], (1,), HIST // 2, HIST + 1).astype(jnp.int32),
    }


TIME_STEP = 0.2
COUPLING = 5.0
DRIVE_RATE = 0.3
PRECISE = lax.Precision.HIGHEST


def lattice_tables(momentum_map, side):
    mom_count = momentum_map.shape[0]
    sites = jnp.arange(mom_count, dtype=jnp.int32)
    mom_x = momentum_map // side
    mom_y = momentum_map % side
    site_x = sites // side
    site_y = sites % side
    winding = (site_x[:, None] * mom_x[None, :] + site_y[:, None] * mom_y[None, :]) % side
    phases = winding.astype(jnp.float32) * (2.0 * jnp.pi / side)
    return jnp.cos(phases), jnp.sin(phases)


def band_energy(own_map, row_times, side):
    wave_x = (own_map // side).astype(jnp.float32) * (2.0 * jnp.pi / side)
    wave_y = (own_map % side).astype(jnp.float32) * (2.0 * jnp.pi / side)
    drift = DRIVE_RATE * row_times
    return -2.0 * (jnp.cos(wave_x[:, None] + drift[None, :]) + jnp.cos(wave_y[:, None] + drift[None, :]))


def to_sites(cosine_table, sine_table, lattice):
    mom_count = lattice.shape[1]
    paired = lattice.reshape(2, 2, mom_count, lattice.shape[2])
    parts_re = paired[:, 0]
    parts_im = paired[:, 1]

    def apply_table(table, values):
        return jnp.einsum("rk,wkc->wrc", table, values, precision=PRECISE)

    site_re = (apply_table(cosine_table, parts_re) - apply_table(sine_table, parts_im)) / mom_count
    site_im = (apply_table(cosine_table, parts_im) + apply_table(sine_table, parts_re)) / mom_count
    return jnp.stack([site_re, site_im], axis=1).reshape(4, cosine_table.shape[0], lattice.shape[2])


def from_sites(cosine_table, sine_table, lattice):
    paired = lattice.reshape(2, 2, lattice.shape[1], lattice.shape[2])
    parts_re = paired[:, 0]
    parts_im = paired[:, 1]

    def apply_table(table, values):
        return jnp.einsum("rk,wrc->wkc", table, values, precision=PRECISE)

    mom_re = apply_table(cosine_table, parts_re) + apply_table(sine_table, parts_im)
    mom_im = apply_table(cosine_table, parts_im) - apply_table(sine_table, parts_re)
    return jnp.stack([mom_re, mom_im], axis=1).reshape(4, cosine_table.shape[1], lattice.shape[2])


def bubble_term(left_re, left_im, right_re, right_im):
    square_re = left_re * left_re - left_im * left_im
    square_im = 2.0 * left_re * left_im
    factor = -COUPLING * COUPLING
    return factor * (square_re * right_re + square_im * right_im), factor * (square_im * right_re - square_re * right_im)


def bubble(lattice):
    ret_re, ret_im, less_re, less_im = lattice[0], lattice[1], lattice[2], lattice[3]
    great_re = less_re + ret_re
    great_im = less_im + ret_im
    lesser_re, lesser_im = bubble_term(less_re, less_im, great_re, great_im)
    greater_re, greater_im = bubble_term(great_re, great_im, less_re, less_im)
    return jnp.stack([greater_re - lesser_re, greater_im - lesser_im, lesser_re, lesser_im])


def contract(energy_pair, stored_pair):
    product = jnp.einsum("akiu,bkus->abkis", energy_pair, stored_pair, precision=PRECISE)
    return product[0, 0] - product[1, 1], product[0, 1] + product[1, 0]


def memory_integral(self_energy, history):
    ret_ret = contract(self_energy[0:2], history[0])
    ret_less = contract(self_energy[0:2], history[1])
    less_adv = contract(self_energy[2:4], history[2])
    return TIME_STEP * jnp.stack([ret_ret[0], ret_ret[1], ret_less[0] + less_adv[0], ret_less[1] + less_adv[1]])


def rotate(total):
    return jnp.stack([total[1], -total[0], total[3], -total[2]])


def reference(new_rows, history, momentum_map, step_index, history_len):
    mom_count = new_rows.shape[1]
    row_count = new_rows.shape[2]
    time_count = new_rows.shape[3]
    cosine_table, sine_table = lattice_tables(momentum_map, SIDE)
    memory_mask = (jnp.arange(time_count, dtype=jnp.int32) < history_len[0]).astype(jnp.float32)
    first_times = step_index[0].astype(jnp.float32) + jnp.arange(row_count, dtype=jnp.int32).astype(jnp.float32)

    def slope(estimate, offset_steps):
        band = band_energy(momentum_map, (first_times + offset_steps) * TIME_STEP, SIDE)
        lattice = to_sites(cosine_table, sine_table, estimate.reshape(4, mom_count, row_count * time_count))
        self_energy = from_sites(cosine_table, sine_table, bubble(lattice))
        self_energy = self_energy.reshape(4, mom_count, row_count, time_count) * memory_mask
        integral = memory_integral(self_energy, history)
        return rotate(band[None, :, :, None] * estimate + integral)

    current = new_rows
    for time_step in range(2):
        slope_now = slope(current, float(time_step))
        estimate = current + TIME_STEP * slope_now
        for corrector in range(2):
            estimate = current + 0.5 * TIME_STEP * (slope_now + slope(estimate, float(time_step + 1)))
        current = estimate
    return current
```

```python
import functools

import jax
import jax.numpy as jnp
from jax import lax
from jax.experimental import pallas as pl
from jax.experimental.pallas import tpu as pltpu
from jax.sharding import PartitionSpec as P


SIDE = 16


TIME_STEP = 0.2
COUPLING = 5.0
DRIVE_RATE = 0.3
PRECISE = lax.Precision.HIGHEST


def lattice_tables(momentum_map, side):
    mom_count = momentum_map.shape[0]
    sites = jnp.arange(mom_count, dtype=jnp.int32)
    mom_x = momentum_map // side
    mom_y = momentum_map % side
    site_x = sites // side
    site_y = sites % side
    winding = (site_x[:, None] * mom_x[None, :] + site_y[:, None] * mom_y[None, :]) % side
    phases = winding.astype(jnp.float32) * (2.0 * jnp.pi / side)
    return (jnp.cos(phases), jnp.sin(phases))


def band_energy(own_map, row_times, side):
    wave_x = (own_map // side).astype(jnp.float32) * (2.0 * jnp.pi / side)
    wave_y = (own_map % side).astype(jnp.float32) * (2.0 * jnp.pi / side)
    drift = DRIVE_RATE * row_times
    return -2.0 * (
        jnp.cos(wave_x[:, None] + drift[None, :]) + jnp.cos(wave_y[:, None] + drift[None, :])
    )


def to_sites(cosine_table, sine_table, lattice):
    mom_count = lattice.shape[1]
    paired = lattice.reshape(2, 2, mom_count, lattice.shape[2])
    parts_re = paired[:, 0]
    parts_im = paired[:, 1]

    def apply_table(table, values):
        return jnp.einsum("rk,wkc->wrc", table, values, precision=PRECISE)

    site_re = (apply_table(cosine_table, parts_re) - apply_table(sine_table, parts_im)) / mom_count
    site_im = (apply_table(cosine_table, parts_im) + apply_table(sine_table, parts_re)) / mom_count
    return jnp.stack([site_re, site_im], axis=1).reshape(4, cosine_table.shape[0], lattice.shape[2])


def from_sites(cosine_table, sine_table, lattice):
    paired = lattice.reshape(2, 2, lattice.shape[1], lattice.shape[2])
    parts_re = paired[:, 0]
    parts_im = paired[:, 1]

    def apply_table(table, values):
        return jnp.einsum("rk,wrc->wkc", table, values, precision=PRECISE)

    mom_re = apply_table(cosine_table, parts_re) + apply_table(sine_table, parts_im)
    mom_im = apply_table(cosine_table, parts_im) - apply_table(sine_table, parts_re)
    return jnp.stack([mom_re, mom_im], axis=1).reshape(4, cosine_table.shape[1], lattice.shape[2])


def bubble_term(left_re, left_im, right_re, right_im):
    square_re = left_re * left_re - left_im * left_im
    square_im = 2.0 * left_re * left_im
    factor = -COUPLING * COUPLING
    return (
        factor * (square_re * right_re + square_im * right_im),
        factor * (square_im * right_re - square_re * right_im),
    )


def bubble(lattice):
    ret_re, ret_im, less_re, less_im = (lattice[0], lattice[1], lattice[2], lattice[3])
    great_re = less_re + ret_re
    great_im = less_im + ret_im
    lesser_re, lesser_im = bubble_term(less_re, less_im, great_re, great_im)
    greater_re, greater_im = bubble_term(great_re, great_im, less_re, less_im)
    return jnp.stack([greater_re - lesser_re, greater_im - lesser_im, lesser_re, lesser_im])


def contract(energy_pair, stored_pair):
    product = jnp.einsum("akiu,bkus->abkis", energy_pair, stored_pair, precision=PRECISE)
    return (product[0, 0] - product[1, 1], product[0, 1] + product[1, 0])


def memory_integral(self_energy, history):
    ret_ret = contract(self_energy[0:2], history[0])
    ret_less = contract(self_energy[0:2], history[1])
    less_adv = contract(self_energy[2:4], history[2])
    return TIME_STEP * jnp.stack(
        [ret_ret[0], ret_ret[1], ret_less[0] + less_adv[0], ret_less[1] + less_adv[1]]
    )


def rotate(total):
    return jnp.stack([total[1], -total[0], total[3], -total[2]])


def body(new_rows, history, momentum_map, step_index, history_len):
    own_count = new_rows.shape[1]
    row_count = new_rows.shape[2]
    time_count = new_rows.shape[3]
    cosine_table, sine_table = lattice_tables(momentum_map, SIDE)
    mom_start = lax.axis_index("mom") * own_count
    own_map = lax.dynamic_slice_in_dim(momentum_map, mom_start, own_count, 0)
    time_start = lax.axis_index("tm") * time_count
    positions = time_start + jnp.arange(time_count, dtype=jnp.int32)
    memory_mask = (positions < history_len[0]).astype(jnp.float32)
    first_times = step_index[0].astype(jnp.float32) + jnp.arange(row_count, dtype=jnp.int32).astype(
        jnp.float32
    )

    def slope(estimate, offset_steps):
        band = band_energy(own_map, (first_times + offset_steps) * TIME_STEP, SIDE)
        flattened = estimate.reshape(4, own_count, row_count * time_count)
        by_site = lax.all_to_all(flattened, "mom", split_axis=2, concat_axis=1, tiled=True)
        site_energy = from_sites(
            cosine_table, sine_table, bubble(to_sites(cosine_table, sine_table, by_site))
        )
        returned = lax.all_to_all(site_energy, "mom", split_axis=1, concat_axis=2, tiled=True)
        self_energy = returned.reshape(4, own_count, row_count, time_count)
        self_energy = self_energy * memory_mask
        partial_rows = memory_integral(self_energy, history)
        integral = lax.psum_scatter(partial_rows, "tm", scatter_dimension=3, tiled=True)
        return rotate(band[None, :, :, None] * estimate + integral)

    current = new_rows
    for time_step in range(2):
        slope_now = slope(current, float(time_step))
        estimate = current + TIME_STEP * slope_now
        for corrector in range(2):
            estimate = current + 0.5 * TIME_STEP * (
                slope_now + slope(estimate, float(time_step + 1))
            )
        current = estimate
    return current


MESH = pl.DeviceIdType.MESH
CHUNKS = 4


def halves(values):
    high = values.astype(jnp.bfloat16)
    return high, (values - high.astype(jnp.float32)).astype(jnp.bfloat16)


def product(left, right):
    return jnp.dot(left, right, preferred_element_type=jnp.float32)


def triple(left_high, left_low, right):
    right_high, right_low = halves(right)
    return (
        product(left_high, right_high)
        + product(left_high, right_low)
        + product(left_low, right_high)
    )


def integral_kernel(
    mom_size,
    slots,
    state_ref,
    mask_ref,
    site_high,
    site_low,
    back_high,
    back_low,
    history_ref,
    out_ref,
    outgoing,
    gathered,
    energy,
    returned,
    partial,
    core_rows,
    chip_rows,
    stored,
    stored_sem,
    row_send,
    row_recv,
    energy_send,
    energy_recv,
    core_send,
    core_recv,
    chip_send,
    chip_recv,
):
    mom = lax.axis_index("mom")
    tm = lax.axis_index("tm")
    core = tm % 2
    chip = tm // 2
    near = chip * 2 + (1 - core)
    far = (1 - chip) * 2 + core
    _, own, rows, times = out_ref.shape
    share = rows // mom_size
    sites = gathered.shape[2]
    chunk = own // CHUNKS

    def fetch(index, slot):
        return pltpu.make_async_copy(
            history_ref.at[:, :, index], stored.at[slot], stored_sem.at[slot]
        )

    for slot in range(slots):
        fetch(slot, slot).start()

    barrier = pltpu.get_barrier_semaphore()
    for step in range(1, mom_size):
        pl.semaphore_signal(
            barrier, inc=1, device_id={"mom": (mom + step) % mom_size}, device_id_type=MESH
        )
    for peer in (near, far):
        pl.semaphore_signal(barrier, inc=1, device_id={"tm": peer}, device_id_type=MESH)

    @pl.loop(0, rows)
    def _(row):
        for part in range(4):
            outgoing[row, part] = state_ref[pl.ds(part * own * rows + row, own, stride=rows), :]

    pl.semaphore_wait(barrier, mom_size + 1)

    def row_copy(line, step):
        peer = (mom + step) % mom_size
        return pltpu.make_async_remote_copy(
            src_ref=outgoing.at[peer * share + line],
            dst_ref=gathered.at[line, :, pl.ds(pl.multiple_of(mom * own, own), own), :],
            send_sem=row_send.at[line, step],
            recv_sem=row_recv.at[line, step],
            device_id={"mom": peer},
            device_id_type=MESH,
        )

    def landing(line):
        depth = 4 * own
        return pl.ds(pl.multiple_of((mom * share + line) * depth, depth), depth)

    def energy_copy(line, step):
        peer = (mom + step) % mom_size
        return pltpu.make_async_remote_copy(
            src_ref=energy.at[line, peer],
            dst_ref=returned.at[landing(line)],
            send_sem=energy_send.at[line, step],
            recv_sem=energy_recv.at[line, step],
            device_id={"mom": peer},
            device_id_type=MESH,
        )

    for line in range(share):
        for step in range(1, mom_size):
            row_copy(line, step).start()
    mine = pl.ds(pl.multiple_of(mom * own, own), own)
    for line in range(share):
        gathered[line, :, mine, :] = outgoing[mom * share + line]

    mask = mask_ref[0:1, :]

    @pl.loop(0, share)
    def _(line):
        for step in range(1, mom_size):
            row_copy(line, step).wait_recv()
        fields = []
        for pair in range(2):
            both = jnp.concatenate(
                [gathered[line, 2 * pair], gathered[line, 2 * pair + 1]], axis=1
            )
            turned = triple(site_high[...], site_low[...], both)
            fields.append((turned[:sites, :times] - turned[sites:, times:]) / sites)
            fields.append((turned[:sites, times:] + turned[sites:, :times]) / sites)
        ret_re, ret_im, less_re, less_im = fields
        great_re = less_re + ret_re
        great_im = less_im + ret_im
        lesser_re, lesser_im = bubble_term(less_re, less_im, great_re, great_im)
        greater_re, greater_im = bubble_term(great_re, great_im, less_re, less_im)
        pairs = (
            (greater_re - lesser_re, greater_im - lesser_im),
            (lesser_re, lesser_im),
        )
        for pair, (part_re, part_im) in enumerate(pairs):
            both = jnp.concatenate([part_re, part_im], axis=1)
            turned = triple(back_high[...], back_low[...], both)
            mom_re = (turned[:sites, :times] + turned[sites:, times:]) * mask
            mom_im = (turned[:sites, times:] - turned[sites:, :times]) * mask
            for part, values in ((2 * pair, mom_re), (2 * pair + 1, mom_im)):
                for peer in range(mom_size):
                    energy[line, peer, part * own : (part + 1) * own] = values[
                        peer * own : (peer + 1) * own
                    ]
        for step in range(1, mom_size):
            energy_copy(line, step).start()
        returned[landing(line)] = energy[line, mom]

    for line in range(share):
        for step in range(1, mom_size):
            energy_copy(line, step).wait_recv()

    def one_momentum(index):
        slot = index % slots
        fetch(index, slot).wait()
        ret_re, ret_im, less_re, less_im = [
            returned[pl.ds(part * own + index, rows, stride=4 * own), :] for part in range(4)
        ]

        def folded(part_re, part_im):
            return jnp.concatenate(
                [
                    jnp.concatenate([part_re, -part_im], axis=1),
                    jnp.concatenate([part_im, part_re], axis=1),
                ],
                axis=0,
            )

        def applied(high, both, kind):
            weights_high, weights_low = halves(stored[slot, kind].reshape(2 * times, -1))
            stacked = product(both, weights_high)
            return stacked[: 2 * rows] + stacked[2 * rows :] + product(high, weights_low)

        ret_high, ret_low = halves(folded(ret_re, ret_im))
        ret_both = jnp.concatenate([ret_high, ret_low], axis=0)
        less_high, less_low = halves(folded(less_re, less_im))
        less_both = jnp.concatenate([less_high, less_low], axis=0)
        ret_sum = applied(ret_high, ret_both, 0)
        less_sum = applied(ret_high, ret_both, 1) + applied(less_high, less_both, 2)
        for block in range(4):
            window = slice(block * times, (block + 1) * times)
            partial[block, index, : 2 * rows] = TIME_STEP * ret_sum[:, window]
            partial[block, index, 2 * rows :] = TIME_STEP * less_sum[:, window]

        @pl.when(index + slots < own)
        def _():
            fetch(index + slots, slot).start()

    def core_copy(piece, side):
        span = pl.ds(piece * chunk, chunk)
        return pltpu.make_async_remote_copy(
            src_ref=partial.at[2 * side + (1 - core), span],
            dst_ref=core_rows.at[side, span],
            send_sem=core_send.at[side, piece],
            recv_sem=core_recv.at[side, piece],
            device_id={"tm": near},
            device_id_type=MESH,
        )

    def chip_copy(piece):
        span = pl.ds(piece * chunk, chunk)
        return pltpu.make_async_remote_copy(
            src_ref=partial.at[2 * (1 - chip) + core, span],
            dst_ref=chip_rows.at[span],
            send_sem=chip_send.at[piece],
            recv_sem=chip_recv.at[piece],
            device_id={"tm": far},
            device_id_type=MESH,
        )

    @pl.loop(0, CHUNKS + 2)
    def _(turn):
        @pl.when(turn < CHUNKS)
        def _():
            @pl.loop(0, chunk)
            def _(inner):
                one_momentum(turn * chunk + inner)

            for side in range(2):
                core_copy(turn, side).start()

        @pl.when((turn >= 1) & (turn <= CHUNKS))
        def _():
            piece = turn - 1
            span = pl.ds(piece * chunk, chunk)
            for side in range(2):
                core_copy(piece, side).wait_recv()
                block = 2 * side + core
                partial[block, span] = partial[block, span] + core_rows[side, span]
            chip_copy(piece).start()

        @pl.when(turn >= 2)
        def _():
            piece = turn - 2
            span = pl.ds(piece * chunk, chunk)
            chip_copy(piece).wait_recv()
            total = partial[2 * chip + core, span] + chip_rows[span]
            for part in range(4):
                out_ref[part, span] = total[:, part * rows : (part + 1) * rows, :]

    for line in range(share):
        for step in range(1, mom_size):
            row_copy(line, step).wait_send()
            energy_copy(line, step).wait_send()
    for piece in range(CHUNKS):
        for side in range(2):
            core_copy(piece, side).wait_send()
        chip_copy(piece).wait_send()


def fits(mesh_sizes, new_rows):
    _, own_count, row_count, time_count = new_rows.shape
    return (
        mesh_sizes["tm"] == 4
        and row_count % mesh_sizes["mom"] == 0
        and row_count % 8 == 0
        and own_count % 8 == 0
        and time_count % 128 == 0
    )


def slope_integral(mom_size, estimate, mask_rows, tables, history):
    parts, own, rows, times = estimate.shape
    sites = own * mom_size
    full = history.shape[4]
    share = rows // mom_size
    slots = min(16, own)
    vmem = pl.BlockSpec(memory_space=pltpu.VMEM)
    dma = pltpu.SemaphoreType.DMA
    f32 = jnp.float32
    return pl.pallas_call(
        functools.partial(integral_kernel, mom_size, slots),
        out_shape=jax.ShapeDtypeStruct(estimate.shape, f32),
        in_specs=[vmem] * 6 + [pl.BlockSpec(memory_space=pl.ANY)],
        out_specs=vmem,
        scratch_shapes=[
            pltpu.VMEM((rows, parts, own, times), f32),
            pltpu.VMEM((share, parts, sites, times), f32),
            pltpu.VMEM((share, mom_size, parts * own, times), f32),
            pltpu.VMEM((rows * parts * own, times), f32),
            pltpu.VMEM((4, own, parts * rows, times), f32),
            pltpu.VMEM((2, own, parts * rows, times), f32),
            pltpu.VMEM((own, parts * rows, times), f32),
            pltpu.VMEM((slots, 3, 2, times, full), f32),
            dma((slots,)),
            dma((share, mom_size)),
            dma((share, mom_size)),
            dma((share, mom_size)),
            dma((share, mom_size)),
            dma((2, CHUNKS)),
            dma((2, CHUNKS)),
            dma((CHUNKS,)),
            dma((CHUNKS,)),
        ],
        compiler_params=pltpu.CompilerParams(
            collective_id=0, has_side_effects=True, vmem_limit_bytes=56 * 1024 * 1024
        ),
        name="slope_integral",
    )(estimate.reshape(parts * own * rows, times), mask_rows, *tables, history)


def table_halves(table):
    high = lax.reduce_precision(table, exponent_bits=8, mantissa_bits=7)
    return high.astype(jnp.bfloat16), (table - high).astype(jnp.bfloat16)


def fused_body(mom_size, new_rows, history, momentum_map, step_index, history_len):
    own_count = new_rows.shape[1]
    row_count = new_rows.shape[2]
    time_count = new_rows.shape[3]
    cosine_table, sine_table = lattice_tables(momentum_map, SIDE)
    tables = table_halves(jnp.concatenate([cosine_table, sine_table], axis=0)) + table_halves(
        jnp.concatenate([cosine_table.T, sine_table.T], axis=0)
    )
    own_map = lax.dynamic_slice_in_dim(momentum_map, lax.axis_index("mom") * own_count, own_count, 0)
    positions = lax.axis_index("tm") * time_count + jnp.arange(time_count, dtype=jnp.int32)
    memory_mask = (positions < history_len[0]).astype(jnp.float32)
    mask_rows = jnp.broadcast_to(memory_mask[None, :], (8, time_count))
    first_times = step_index[0].astype(jnp.float32) + jnp.arange(row_count, dtype=jnp.int32).astype(
        jnp.float32
    )

    def slope(estimate, offset_steps):
        band = band_energy(own_map, (first_times + offset_steps) * TIME_STEP, SIDE)
        integral = slope_integral(mom_size, estimate, mask_rows, tables, history)
        return rotate(band[None, :, :, None] * estimate + integral)

    current = new_rows
    for time_step in range(2):
        slope_now = slope(current, float(time_step))
        estimate = current + TIME_STEP * slope_now
        for corrector in range(2):
            estimate = current + 0.5 * TIME_STEP * (
                slope_now + slope(estimate, float(time_step + 1))
            )
        current = estimate
    return current


def solution(mesh):
    in_specs = (P(None, "mom", None, "tm"), P(None, None, "mom", "tm", None), P(), P(), P())
    out_specs = P(None, "mom", None, "tm")

    def dispatch(new_rows, *others):
        if fits(dict(mesh.shape), new_rows):
            return fused_body(mesh.shape["mom"], new_rows, *others)
        return body(new_rows, *others)

    return jax.shard_map(
        dispatch, mesh=mesh, in_specs=in_specs, out_specs=out_specs, check_vma=False
    )
```

```python
import functools

import jax
import jax.numpy as jnp
from jax import lax
from jax.experimental import pallas as pl
from jax.experimental.pallas import tpu as pltpu
from jax.sharding import PartitionSpec as P


SIDE = 16


TIME_STEP = 0.2
COUPLING = 5.0
DRIVE_RATE = 0.3
PRECISE = lax.Precision.HIGHEST


def lattice_tables(momentum_map, side):
    mom_count = momentum_map.shape[0]
    sites = jnp.arange(mom_count, dtype=jnp.int32)
    mom_x = momentum_map // side
    mom_y = momentum_map % side
    site_x = sites // side
    site_y = sites % side
    winding = (site_x[:, None] * mom_x[None, :] + site_y[:, None] * mom_y[None, :]) % side
    phases = winding.astype(jnp.float32) * (2.0 * jnp.pi / side)
    return (jnp.cos(phases), jnp.sin(phases))


def band_energy(own_map, row_times, side):
    wave_x = (own_map // side).astype(jnp.float32) * (2.0 * jnp.pi / side)
    wave_y = (own_map % side).astype(jnp.float32) * (2.0 * jnp.pi / side)
    drift = DRIVE_RATE * row_times
    return -2.0 * (
        jnp.cos(wave_x[:, None] + drift[None, :]) + jnp.cos(wave_y[:, None] + drift[None, :])
    )


def to_sites(cosine_table, sine_table, lattice):
    mom_count = lattice.shape[1]
    paired = lattice.reshape(2, 2, mom_count, lattice.shape[2])
    parts_re = paired[:, 0]
    parts_im = paired[:, 1]

    def apply_table(table, values):
        return jnp.einsum("rk,wkc->wrc", table, values, precision=PRECISE)

    site_re = (apply_table(cosine_table, parts_re) - apply_table(sine_table, parts_im)) / mom_count
    site_im = (apply_table(cosine_table, parts_im) + apply_table(sine_table, parts_re)) / mom_count
    return jnp.stack([site_re, site_im], axis=1).reshape(4, cosine_table.shape[0], lattice.shape[2])


def from_sites(cosine_table, sine_table, lattice):
    paired = lattice.reshape(2, 2, lattice.shape[1], lattice.shape[2])
    parts_re = paired[:, 0]
    parts_im = paired[:, 1]

    def apply_table(table, values):
        return jnp.einsum("rk,wrc->wkc", table, values, precision=PRECISE)

    mom_re = apply_table(cosine_table, parts_re) + apply_table(sine_table, parts_im)
    mom_im = apply_table(cosine_table, parts_im) - apply_table(sine_table, parts_re)
    return jnp.stack([mom_re, mom_im], axis=1).reshape(4, cosine_table.shape[1], lattice.shape[2])


def bubble_term(left_re, left_im, right_re, right_im):
    square_re = left_re * left_re - left_im * left_im
    square_im = 2.0 * left_re * left_im
    factor = -COUPLING * COUPLING
    return (
        factor * (square_re * right_re + square_im * right_im),
        factor * (square_im * right_re - square_re * right_im),
    )


def bubble(lattice):
    ret_re, ret_im, less_re, less_im = (lattice[0], lattice[1], lattice[2], lattice[3])
    great_re = less_re + ret_re
    great_im = less_im + ret_im
    lesser_re, lesser_im = bubble_term(less_re, less_im, great_re, great_im)
    greater_re, greater_im = bubble_term(great_re, great_im, less_re, less_im)
    return jnp.stack([greater_re - lesser_re, greater_im - lesser_im, lesser_re, lesser_im])


def contract(energy_pair, stored_pair):
    product = jnp.einsum("akiu,bkus->abkis", energy_pair, stored_pair, precision=PRECISE)
    return (product[0, 0] - product[1, 1], product[0, 1] + product[1, 0])


def memory_integral(self_energy, history):
    ret_ret = contract(self_energy[0:2], history[0])
    ret_less = contract(self_energy[0:2], history[1])
    less_adv = contract(self_energy[2:4], history[2])
    return TIME_STEP * jnp.stack(
        [ret_ret[0], ret_ret[1], ret_less[0] + less_adv[0], ret_less[1] + less_adv[1]]
    )


def rotate(total):
    return jnp.stack([total[1], -total[0], total[3], -total[2]])


def body(new_rows, history, momentum_map, step_index, history_len):
    own_count = new_rows.shape[1]
    row_count = new_rows.shape[2]
    time_count = new_rows.shape[3]
    cosine_table, sine_table = lattice_tables(momentum_map, SIDE)
    mom_start = lax.axis_index("mom") * own_count
    own_map = lax.dynamic_slice_in_dim(momentum_map, mom_start, own_count, 0)
    time_start = lax.axis_index("tm") * time_count
    positions = time_start + jnp.arange(time_count, dtype=jnp.int32)
    memory_mask = (positions < history_len[0]).astype(jnp.float32)
    first_times = step_index[0].astype(jnp.float32) + jnp.arange(row_count, dtype=jnp.int32).astype(
        jnp.float32
    )

    def slope(estimate, offset_steps):
        band = band_energy(own_map, (first_times + offset_steps) * TIME_STEP, SIDE)
        flattened = estimate.reshape(4, own_count, row_count * time_count)
        by_site = lax.all_to_all(flattened, "mom", split_axis=2, concat_axis=1, tiled=True)
        site_energy = from_sites(
            cosine_table, sine_table, bubble(to_sites(cosine_table, sine_table, by_site))
        )
        returned = lax.all_to_all(site_energy, "mom", split_axis=1, concat_axis=2, tiled=True)
        self_energy = returned.reshape(4, own_count, row_count, time_count)
        self_energy = self_energy * memory_mask
        partial_rows = memory_integral(self_energy, history)
        integral = lax.psum_scatter(partial_rows, "tm", scatter_dimension=3, tiled=True)
        return rotate(band[None, :, :, None] * estimate + integral)

    current = new_rows
    for time_step in range(2):
        slope_now = slope(current, float(time_step))
        estimate = current + TIME_STEP * slope_now
        for corrector in range(2):
            estimate = current + 0.5 * TIME_STEP * (
                slope_now + slope(estimate, float(time_step + 1))
            )
        current = estimate
    return current


MESH = pl.DeviceIdType.MESH
CHUNKS = 8


def halves(values):
    high = values.astype(jnp.bfloat16)
    return high, (values - high.astype(jnp.float32)).astype(jnp.bfloat16)


def product(left, right):
    return jnp.dot(left, right, preferred_element_type=jnp.float32)


def triple(left_high, left_low, right):
    right_high, right_low = halves(right)
    return (
        product(left_high, right_high)
        + product(left_high, right_low)
        + product(left_low, right_high)
    )


def integral_kernel(
    mom_size,
    slots,
    state_ref,
    mask_ref,
    site_high,
    site_low,
    back_high,
    back_low,
    history_ref,
    out_ref,
    outgoing,
    gathered,
    energy,
    returned,
    partial,
    core_rows,
    chip_rows,
    stored,
    stored_sem,
    row_send,
    row_recv,
    energy_send,
    energy_recv,
    core_send,
    core_recv,
    chip_send,
    chip_recv,
):
    mom = lax.axis_index("mom")
    tm = lax.axis_index("tm")
    core = tm % 2
    chip = tm // 2
    near = chip * 2 + (1 - core)
    far = (1 - chip) * 2 + core
    _, own, rows, times = out_ref.shape
    share = rows // mom_size
    sites = gathered.shape[2]
    chunk = own // CHUNKS

    def fetch(index, slot):
        return pltpu.make_async_copy(
            history_ref.at[:, :, index], stored.at[slot], stored_sem.at[slot]
        )

    for slot in range(slots):
        fetch(slot, slot).start()

    barrier = pltpu.get_barrier_semaphore()
    for step in range(1, mom_size):
        pl.semaphore_signal(
            barrier, inc=1, device_id={"mom": (mom + step) % mom_size}, device_id_type=MESH
        )
    for peer in (near, far):
        pl.semaphore_signal(barrier, inc=1, device_id={"tm": peer}, device_id_type=MESH)

    @pl.loop(0, rows)
    def _(row):
        for part in range(4):
            outgoing[row, part] = state_ref[pl.ds(part * own * rows + row, own, stride=rows), :]

    pl.semaphore_wait(barrier, mom_size + 1)

    def row_copy(line, step):
        peer = (mom + step) % mom_size
        return pltpu.make_async_remote_copy(
            src_ref=outgoing.at[line * mom_size + peer],
            dst_ref=gathered.at[line, :, pl.ds(pl.multiple_of(mom * own, own), own), :],
            send_sem=row_send.at[line, step],
            recv_sem=row_recv.at[line, step],
            device_id={"mom": peer},
            device_id_type=MESH,
        )

    def landing(line):
        depth = 4 * own
        return pl.ds(pl.multiple_of((line * mom_size + mom) * depth, depth), depth)

    def energy_copy(line, step):
        peer = (mom + step) % mom_size
        return pltpu.make_async_remote_copy(
            src_ref=energy.at[line, peer],
            dst_ref=returned.at[landing(line)],
            send_sem=energy_send.at[line, step],
            recv_sem=energy_recv.at[line, step],
            device_id={"mom": peer},
            device_id_type=MESH,
        )

    for line in range(share):
        for step in range(1, mom_size):
            row_copy(line, step).start()
    mine = pl.ds(pl.multiple_of(mom * own, own), own)
    for line in range(share):
        gathered[line, :, mine, :] = outgoing[line * mom_size + mom]

    mask = mask_ref[0:1, :]

    @pl.loop(0, share)
    def _(line):
        for step in range(1, mom_size):
            row_copy(line, step).wait_recv()
        fields = []
        for pair in range(2):
            both = jnp.concatenate(
                [gathered[line, 2 * pair], gathered[line, 2 * pair + 1]], axis=1
            )
            turned = triple(site_high[...], site_low[...], both)
            fields.append((turned[:sites, :times] - turned[sites:, times:]) / sites)
            fields.append((turned[:sites, times:] + turned[sites:, :times]) / sites)
        ret_re, ret_im, less_re, less_im = fields
        great_re = less_re + ret_re
        great_im = less_im + ret_im
        lesser_re, lesser_im = bubble_term(less_re, less_im, great_re, great_im)
        greater_re, greater_im = bubble_term(great_re, great_im, less_re, less_im)
        pairs = (
            (greater_re - lesser_re, greater_im - lesser_im),
            (lesser_re, lesser_im),
        )
        for pair, (part_re, part_im) in enumerate(pairs):
            both = jnp.concatenate([part_re, part_im], axis=1)
            turned = triple(back_high[...], back_low[...], both)
            mom_re = (turned[:sites, :times] + turned[sites:, times:]) * mask
            mom_im = (turned[:sites, times:] - turned[sites:, :times]) * mask
            for part, values in ((2 * pair, mom_re), (2 * pair + 1, mom_im)):
                for peer in range(mom_size):
                    energy[line, peer, part * own : (part + 1) * own] = values[
                        peer * own : (peer + 1) * own
                    ]
        for step in range(1, mom_size):
            energy_copy(line, step).start()
        returned[landing(line)] = energy[line, mom]

    def one_momentum(line, step):
        load = step - line * slots
        index = load % own
        slot = load % slots

        @pl.when((line == 0) | (load >= own))
        def _():
            fetch(index, slot).wait()

        ret_re, ret_im, less_re, less_im = [
            returned[
                pl.ds(line * mom_size * 4 * own + part * own + index, mom_size, stride=4 * own), :
            ]
            for part in range(4)
        ]

        def folded(part_re, part_im):
            return jnp.concatenate(
                [
                    jnp.concatenate([part_re, -part_im], axis=1),
                    jnp.concatenate([part_im, part_re], axis=1),
                ],
                axis=0,
            )

        def applied(high, both, kind):
            weights_high, weights_low = halves(stored[slot, kind].reshape(2 * times, -1))
            stacked = product(both, weights_high)
            return stacked[: 2 * mom_size] + stacked[2 * mom_size :] + product(high, weights_low)

        ret_high, ret_low = halves(folded(ret_re, ret_im))
        ret_both = jnp.concatenate([ret_high, ret_low], axis=0)
        less_high, less_low = halves(folded(less_re, less_im))
        less_both = jnp.concatenate([less_high, less_low], axis=0)
        ret_sum = applied(ret_high, ret_both, 0)
        less_sum = applied(ret_high, ret_both, 1) + applied(less_high, less_both, 2)
        for block in range(4):
            window = slice(block * times, (block + 1) * times)
            partial[line, block, index, : 2 * mom_size] = TIME_STEP * ret_sum[:, window]
            partial[line, block, index, 2 * mom_size :] = TIME_STEP * less_sum[:, window]

        @pl.when(load + slots < own + line * (own - slots))
        def _():
            fetch((load + slots) % own, slot).start()

    def place(turn):
        line = turn // CHUNKS
        return line, pl.ds((turn * chunk - line * slots) % own, chunk)

    def core_copy(turn, side):
        line, span = place(turn)
        return pltpu.make_async_remote_copy(
            src_ref=partial.at[line, 2 * side + (1 - core), span],
            dst_ref=core_rows.at[line, side, span],
            send_sem=core_send.at[side, turn],
            recv_sem=core_recv.at[side, turn],
            device_id={"tm": near},
            device_id_type=MESH,
        )

    def chip_copy(turn):
        line, span = place(turn)
        return pltpu.make_async_remote_copy(
            src_ref=partial.at[line, 2 * (1 - chip) + core, span],
            dst_ref=chip_rows.at[line, span],
            send_sem=chip_send.at[turn],
            recv_sem=chip_recv.at[turn],
            device_id={"tm": far},
            device_id_type=MESH,
        )

    turns = share * CHUNKS

    @pl.loop(0, turns + 2)
    def _(turn):
        @pl.when(turn < turns)
        def _():
            line = turn // CHUNKS

            @pl.when(turn % CHUNKS == 0)
            def _():
                for step in range(1, mom_size):
                    energy_copy(line, step).wait_recv()

            @pl.loop(0, chunk)
            def _(inner):
                one_momentum(line, turn * chunk + inner)

            for side in range(2):
                core_copy(turn, side).start()

        @pl.when((turn >= 1) & (turn <= turns))
        def _():
            line, span = place(turn - 1)
            for side in range(2):
                core_copy(turn - 1, side).wait_recv()
                block = 2 * side + core
                partial[line, block, span] = partial[line, block, span] + core_rows[line, side, span]
            chip_copy(turn - 1).start()

        @pl.when(turn >= 2)
        def _():
            line, span = place(turn - 2)
            chip_copy(turn - 2).wait_recv()
            total = partial[line, 2 * chip + core, span] + chip_rows[line, span]
            group = pl.ds(pl.multiple_of(line * mom_size, mom_size), mom_size)
            for part in range(4):
                out_ref[part, span, group, :] = total[:, part * mom_size : (part + 1) * mom_size, :]

    for line in range(share):
        for step in range(1, mom_size):
            row_copy(line, step).wait_send()
            energy_copy(line, step).wait_send()
    for piece in range(turns):
        for side in range(2):
            core_copy(piece, side).wait_send()
        chip_copy(piece).wait_send()


def fits(mesh_sizes, new_rows):
    _, own_count, row_count, time_count = new_rows.shape
    return (
        mesh_sizes["tm"] == 4
        and mesh_sizes["mom"] % 8 == 0
        and row_count == 2 * mesh_sizes["mom"]
        and own_count % CHUNKS == 0
        and time_count % 128 == 0
    )


def slope_integral(mom_size, estimate, mask_rows, tables, history):
    parts, own, rows, times = estimate.shape
    sites = own * mom_size
    full = history.shape[4]
    share = rows // mom_size
    slots = own - own // CHUNKS
    vmem = pl.BlockSpec(memory_space=pltpu.VMEM)
    dma = pltpu.SemaphoreType.DMA
    f32 = jnp.float32
    return pl.pallas_call(
        functools.partial(integral_kernel, mom_size, slots),
        out_shape=jax.ShapeDtypeStruct(estimate.shape, f32),
        in_specs=[vmem] * 6 + [pl.BlockSpec(memory_space=pl.ANY)],
        out_specs=vmem,
        scratch_shapes=[
            pltpu.VMEM((rows, parts, own, times), f32),
            pltpu.VMEM((share, parts, sites, times), f32),
            pltpu.VMEM((share, mom_size, parts * own, times), f32),
            pltpu.VMEM((rows * parts * own, times), f32),
            pltpu.VMEM((share, 4, own, parts * mom_size, times), f32),
            pltpu.VMEM((share, 2, own, parts * mom_size, times), f32),
            pltpu.VMEM((share, own, parts * mom_size, times), f32),
            pltpu.VMEM((slots, 3, 2, times, full), f32),
            dma((slots,)),
            dma((share, mom_size)),
            dma((share, mom_size)),
            dma((share, mom_size)),
            dma((share, mom_size)),
            dma((2, share * CHUNKS)),
            dma((2, share * CHUNKS)),
            dma((share * CHUNKS,)),
            dma((share * CHUNKS,)),
        ],
        compiler_params=pltpu.CompilerParams(
            collective_id=0, has_side_effects=True, vmem_limit_bytes=60 * 1024 * 1024
        ),
        name="slope_integral",
    )(estimate.reshape(parts * own * rows, times), mask_rows, *tables, history)


def table_halves(table):
    high = lax.reduce_precision(table, exponent_bits=8, mantissa_bits=7)
    return high.astype(jnp.bfloat16), (table - high).astype(jnp.bfloat16)


def fused_body(mom_size, new_rows, history, momentum_map, step_index, history_len):
    own_count = new_rows.shape[1]
    row_count = new_rows.shape[2]
    time_count = new_rows.shape[3]
    cosine_table, sine_table = lattice_tables(momentum_map, SIDE)
    tables = table_halves(jnp.concatenate([cosine_table, sine_table], axis=0)) + table_halves(
        jnp.concatenate([cosine_table.T, sine_table.T], axis=0)
    )
    own_map = lax.dynamic_slice_in_dim(momentum_map, lax.axis_index("mom") * own_count, own_count, 0)
    positions = lax.axis_index("tm") * time_count + jnp.arange(time_count, dtype=jnp.int32)
    memory_mask = (positions < history_len[0]).astype(jnp.float32)
    mask_rows = jnp.broadcast_to(memory_mask[None, :], (8, time_count))
    first_times = step_index[0].astype(jnp.float32) + jnp.arange(row_count, dtype=jnp.int32).astype(
        jnp.float32
    )

    def slope(estimate, offset_steps):
        band = band_energy(own_map, (first_times + offset_steps) * TIME_STEP, SIDE)
        integral = slope_integral(mom_size, estimate, mask_rows, tables, history)
        return rotate(band[None, :, :, None] * estimate + integral)

    current = new_rows
    for time_step in range(2):
        slope_now = slope(current, float(time_step))
        estimate = current + TIME_STEP * slope_now
        for corrector in range(2):
            estimate = current + 0.5 * TIME_STEP * (
                slope_now + slope(estimate, float(time_step + 1))
            )
        current = estimate
    return current


def solution(mesh):
    in_specs = (P(None, "mom", None, "tm"), P(None, None, "mom", "tm", None), P(), P(), P())
    out_specs = P(None, "mom", None, "tm")

    def dispatch(new_rows, *others):
        if fits(dict(mesh.shape), new_rows):
            return fused_body(mesh.shape["mom"], new_rows, *others)
        return body(new_rows, *others)

    return jax.shard_map(
        dispatch, mesh=mesh, in_specs=in_specs, out_specs=out_specs, check_vma=False
    )
```
